32 devices in a mesh: slab: 8 (over y, x, core), group: 4 (over z).
Axes of the slice: x: 2, y: 2, z: 4, core: 2. Of those that a mesh axis runs over, the one named last changes fastest.
Arguments:
- disp_now: float32 [3, 262144], P(None, 'slab'), may hold values from -6 to 6
- disp_prev: float32 [3, 262144], P(None, 'slab'), may hold values from -6 to 6
- inv_mass: float32 [262144], P('slab'), may hold values from 0.5 to 2
- cell_nodes: int32 [1024, 192], P(('slab', 'group')), may hold values from 0 to 98303
- shape_grads: bfloat16 [1024, 3, 192, 128], P(('slab', 'group')), may hold values from -0.125 to 0.125
- cell_weights: float32 [1024, 128], P(('slab', 'group')), may hold values from 0.5 to 2
- cell_shear: float32 [1024], P(('slab', 'group')), may hold values from 0.5 to 2
- cell_bulk: float32 [1024], P(('slab', 'group')), may hold values from 1 to 4
- block_owner: int32 [1024, 1], P(('slab', 'group')), may hold values from 0 to 7; in each aligned block of 32 rows (0 to 31, 32 to 63, ...) at most 4 rows name the same one
- block_nodes: int32 [1024, 256], P(('slab', 'group')), may hold values from 0 to 32767
- block_phi: float32 [1024, 128, 256], P(('slab', 'group')), may hold values from -0.375 to 0.375
- block_corr: float32 [1024, 128, 128], P(('slab', 'group')), may hold values from -0.5 to 0.5
- block_target: float32 [1024, 3, 128], P(('slab', 'group')), may hold values from -6 to 6
- block_fixed: int32 [1024, 128], P(('slab', 'group')), may hold values 0 or 1
Outputs:
- disp_final: float32 [3, 262144], P(None, 'slab')
The draws below stay inside these ranges and needn't reach their ends.
Inputs may be any that keep to these rules, and one draw needn't show every extreme that they name: `cell_nodes`: support node numbers run over the slab below, the cell's own slab and the slab above; those outside the head read zero. `block_owner`: among the 32 blocks of one device at most 4 have one owner slab, and in every draw some device has exactly 4 with one owner.
All inputs are finite; a program needn't handle non-finite values. No bound on the sum of `block_fixed` on one device may be relied on, other than what follows from the above.
Results may differ from the reference program's by a relative error of at most 0.0059.
Values may be sent and summed in bfloat16 or wider, within the bound.
No kernel may reach another device: no remote copies, remote signals or barrier semaphores. Data moves between devices by JAX's collectives and lax.ppermute only.
A program may use at most 192 MiB of HBM per device.

```python
import math
import jax
import jax.numpy as jnp
import numpy as np
from jax import lax

NODE_SLAB = 32768
CELL_DEV = 32
PTS = 128
SUP = 192
BLK_DEV = 32
CAP = 4
BN = 128
BSUP = 256
SLABS = 8
NODES = 262144
CELLS = 1024
BLOCKS = 1024
N_SLAB = 8
N_GROUP = 4


def plant(values, own_key, low, top_value):
    longest = values.shape.index(max(values.shape))
    spots = []
    for shift in (0, 1):
        where = [jax.random.randint(jax.random.fold_in(own_key, axis), (), 0, length) for axis, length in enumerate(values.shape)]
        where[longest] = (where[longest] + shift) % values.shape[longest]
        spots.append(tuple(where))
    return values.at[spots[0]].set(low).at[spots[1]].set(top_value)


def block_levels(key, dims, split, low, top_value):
    factor_of, own = 1.0, jax.random.fold_in(key, 6)
    for dim, shards_of in split:
        heights = jnp.exp(jax.random.uniform(jax.random.fold_in(own, dim), (shards_of,), jnp.float32, low / len(split), top_value / len(split)))
        factor_of = factor_of * jnp.repeat(heights, dims[dim] // shards_of).reshape([-1 if axis == dim else 1 for axis in range(len(dims))])
    return factor_of


def deal_out(stream_key, own, number, rows, count, top, limit, slope):
    sequence = jax.random.permutation(stream_key, count)
    packed, usual = portions_of(count, rows * top, limit, slope, True), portions_of(count, rows * top, limit, slope, False)
    places = jnp.arange(count)

    def named(lengths, turn):
        used = int((lengths > 0).sum())
        fixed = max(1, used // 4)
        moved = fixed + (places - fixed + turn * (used - fixed)) % max(1, count - fixed)
        return jnp.zeros((count,), jnp.int32).at[sequence[jnp.where(places < fixed, places, moved)]].set(jnp.asarray(lengths, jnp.int32))

    lengths = jnp.where(number % 4 == 0, named(packed, number // 4), named(usual, number - number // 4 - 1))
    mixed = jax.random.permutation(jax.random.fold_in(own, 3), count)
    giver, sink = mixed[0:count // 2 * 2:2], mixed[1:count // 2 * 2:2]
    margin = jnp.minimum(lengths[giver] - 1, limit - lengths[sink]) // 2
    margin = jnp.where((giver == sequence[0]) | (sink == sequence[0]) | (lengths[sink] == 0), 0, jnp.maximum(margin, 0))
    moved = jax.random.randint(jax.random.fold_in(own, 4), (count // 2,), 0, 1 << 20) % (margin + 1)
    lengths = lengths.at[giver].add(-moved).at[sink].add(moved)
    labels = jnp.searchsorted(jnp.cumsum(lengths), jnp.arange(rows * top), side="right").astype(jnp.int32)
    table = labels.reshape(top, rows).T
    table = table[jax.random.permutation(jax.random.fold_in(own, 1), rows)]
    turn = jax.random.randint(jax.random.fold_in(own, 2), (rows, 1), 0, top)
    return jnp.take_along_axis(table, (jnp.arange(top)[None, :] + turn) % top, axis=1)


def portions_of(count, total, limit, skew, full):
    portions = [(1 << 20) // math.isqrt(grade ** skew) + 1 for grade in range(1, count + 1)]
    largest = limit if full else min(limit, max(-(-total // count), total * portions[0] // sum(portions)))
    least = 1 if total - largest >= count - 1 else 0
    given, rest = [largest] + [least] * (count - 1), total - largest - least * (count - 1)
    while rest > 0:
        free = [i for i in range(1, count) if given[i] < largest] or [i for i in range(1, count) if given[i] < limit]
        whole, left = sum([portions[i] for i in free]), rest
        for i in free:
            addition = min(limit - given[i], max(1, left * portions[i] // whole), rest)
            given[i] = given[i] + addition
            rest = rest - addition
    return np.array(given)


def normal_values(own_key, shape, deviation, bound, pieces=(), kind=jnp.bfloat16):
    result = deviation * jax.random.normal(own_key, shape, jnp.float32)
    if pieces:
        result = result * block_levels(own_key, shape, pieces, -0.22, 0.18)
    return jnp.clip(result, -bound, bound).astype(kind)


def setup_inputs(seed: int = 0) -> dict:
    seeds = jax.random.split(jax.random.key(seed), 15)
    disp_now = normal_values(seeds[0], (3, NODES), 1.0, 6.0, ((1, 8),), jnp.float32)
    disp_prev = normal_values(seeds[1], (3, NODES), 1.0, 6.0, ((1, 8),), jnp.float32)
    inv_mass = jnp.clip(jnp.exp(math.log(2.0) - 1.3862944 * jax.random.uniform(seeds[2], (NODES,), jnp.float32) ** block_levels(seeds[2], (NODES,), ((0, 8),), -0.2, 0.2)), 0.5, 2.0)
    cell_nodes = plant(jax.random.randint(seeds[3], (CELLS, SUP), 0, 3 * NODE_SLAB), jax.random.fold_in(seeds[3], 1), 0, (3 * NODE_SLAB) - 1).astype(jnp.int32)
    shape_grads = normal_values(seeds[4], (CELLS, 3, SUP, PTS), (SUP * 11) ** -0.5, 0.125, ((0, 32),))
    cell_weights = jnp.clip(jnp.exp(math.log(2.0) - 1.3862944 * jax.random.uniform(seeds[5], (CELLS, PTS), jnp.float32) ** block_levels(seeds[5], (CELLS, PTS), ((0, 32),), -0.2, 0.2)), 0.5, 2.0)
    cell_shear = jnp.clip(jnp.exp(math.log(2.0) - 1.3862944 * jax.random.uniform(seeds[6], (CELLS,), jnp.float32) ** block_levels(seeds[6], (CELLS,), ((0, 32),), -0.2, 0.2)), 0.5, 2.0)
    cell_bulk = jnp.clip(jnp.exp(math.log(4.0) - 1.3862944 * jax.random.uniform(seeds[7], (CELLS,), jnp.float32) ** block_levels(seeds[7], (CELLS,), ((0, 32),), -0.2, 0.2)), 1.0, 4.0)
    block_owner_keys = jax.random.split(jax.random.fold_in(seeds[8], 1), BLOCKS // BLK_DEV)
    block_owner_turns = jax.random.permutation(jax.random.fold_in(seeds[8], 3), BLOCKS // BLK_DEV)
    block_owner = jax.vmap(lambda own, number: deal_out(jax.random.fold_in(seeds[8], 2), own, number, BLK_DEV, SLABS, 1, CAP, 2))(block_owner_keys, block_owner_turns).reshape((BLOCKS, 1))
    block_nodes = plant(jax.random.randint(seeds[9], (BLOCKS, BSUP), 0, NODE_SLAB), jax.random.fold_in(seeds[9], 1), 0, NODE_SLAB - 1).astype(jnp.int32)
    block_phi = normal_values(seeds[10], (BLOCKS, BN, BSUP), BSUP ** -0.5, 0.375, ((0, 32),), jnp.float32)
    block_corr = normal_values(seeds[11], (BLOCKS, BN, BN), BN ** -0.5, 0.5, ((0, 32),), jnp.float32)
    block_target = normal_values(seeds[12], (BLOCKS, 3, BN), 1.0, 6.0, ((0, 32),), jnp.float32)
    block_fixed = plant((jax.random.randint(seeds[13], (BLOCKS, BN), 0, 2) < 1).astype(jnp.int32), jax.random.fold_in(seeds[13], 1), 0, 1)
    return dict(disp_now=disp_now, disp_prev=disp_prev, inv_mass=inv_mass, cell_nodes=cell_nodes, shape_grads=shape_grads, cell_weights=cell_weights, cell_shear=cell_shear, cell_bulk=cell_bulk, block_owner=block_owner, block_nodes=block_nodes, block_phi=block_phi, block_corr=block_corr, block_target=block_target, block_fixed=block_fixed)


def stress_of(grad, shear, bulk):
    identity = jnp.eye(3, dtype=grad.dtype)
    full = grad + identity[None, :, :, None]
    entries = [[full[:, leading, trailing] for trailing in range(3)] for leading in range(3)]
    cofactor = [[entries[(leading + 1) % 3][(trailing + 1) % 3] * entries[(leading + 2) % 3][(trailing + 2) % 3]
                 - entries[(leading + 1) % 3][(trailing + 2) % 3] * entries[(leading + 2) % 3][(trailing + 1) % 3]
                 for trailing in range(3)] for leading in range(3)]
    volume = entries[0][0] * cofactor[0][0] + entries[0][1] * cofactor[0][1] + entries[0][2] * cofactor[0][2]
    clamped = jnp.maximum(volume, 0.3)
    shear_now = shear[:, None]
    factor = (bulk[:, None] * jnp.log(clamped) - shear_now) / clamped
    rows_out = [jnp.stack([shear_now * entries[leading][trailing] + factor * cofactor[leading][trailing]
                           for trailing in range(3)], axis=1) for leading in range(3)]
    return jnp.stack(rows_out, axis=1)


def reference(disp_now, disp_prev, inv_mass, cell_nodes, shape_grads, cell_weights, cell_shear, cell_bulk,
              block_owner, block_nodes, block_phi, block_corr, block_target, block_fixed):
    width = NODE_SLAB
    padded = jnp.pad(disp_now.astype(jnp.bfloat16), ((0, 0), (width, width)))
    per_slab = CELL_DEV * N_GROUP

    def one_slab(total, inputs):
        position, nodes, grads, weights, shear, bulk = inputs
        global_index = (nodes + position * width).astype(jnp.int32)
        gathered = jnp.moveaxis(jnp.take(padded, global_index, axis=1), 0, 1)
        grad = jnp.einsum('cia,cjap->cijp', gathered.astype(jnp.float32), grads.astype(jnp.float32))
        stress = stress_of(grad, shear, bulk)
        weighted = (weights[:, None, None, :] * stress).astype(jnp.bfloat16)
        force = jnp.einsum('cijp,cjap->cia', weighted.astype(jnp.float32), grads.astype(jnp.float32))
        total = total.at[:, global_index].add(jnp.moveaxis(force, 1, 0))
        return total, None

    inputs = (jnp.arange(N_SLAB, dtype=jnp.int32),
              cell_nodes.reshape(N_SLAB, per_slab, SUP),
              shape_grads.reshape((N_SLAB, per_slab) + shape_grads.shape[1:]),
              cell_weights.reshape(N_SLAB, per_slab, PTS),
              cell_shear.reshape(N_SLAB, per_slab),
              cell_bulk.reshape(N_SLAB, per_slab))
    start = jnp.zeros((3, NODES + 2 * width), jnp.float32)
    total, _ = lax.scan(one_slab, start, inputs)
    force_sum = total[:, width:width + NODES]
    disp_next = 2.0 * disp_now - disp_prev - inv_mass[None, :] * force_sum

    block_index = (block_owner[:, 0:1] * width + block_nodes).astype(jnp.int32)
    values = jnp.moveaxis(jnp.take(disp_next, block_index, axis=1), 0, 1)
    highest = lax.Precision.HIGHEST
    interp = jnp.einsum('bma,bia->bim', block_phi, values, precision=highest)
    resid = block_fixed[:, None, :].astype(jnp.float32) * (block_target - interp)
    corr = jnp.einsum('bmq,biq->bim', block_corr, resid, precision=highest)
    delta = jnp.einsum('bma,bim->bia', block_phi, corr, precision=highest)
    added = jnp.zeros((3, NODES), jnp.float32).at[:, block_index].add(jnp.moveaxis(delta, 1, 0))
    return disp_next + added
```

```python
import functools

import jax
import jax.numpy as jnp
from jax import lax
from jax.experimental import pallas as pl
from jax.experimental.pallas import tpu as pltpu
from jax.sharding import PartitionSpec as P

CAP = 4
LANES = 128
GROUP_CELLS = 8
BF = jnp.bfloat16
F32 = jnp.float32
VMEM = pl.BlockSpec(memory_space=pltpu.VMEM)
SMEM = pl.BlockSpec(memory_space=pltpu.SMEM)
PARAMS = pltpu.CompilerParams(vmem_limit_bytes=56 * 1024 * 1024)
NT = (((1,), (1,)), ((), ()))
NN = (((1,), (0,)), ((), ()))


def call(kernel, outs, in_specs, out_specs=None, **extra):
    return pl.pallas_call(
        kernel,
        out_shape=outs,
        in_specs=in_specs,
        out_specs=jax.tree.map(lambda _: VMEM, outs) if out_specs is None else out_specs,
        compiler_params=PARAMS,
        **extra,
    )


def shape_of(dims, dtype):
    return jax.ShapeDtypeStruct(dims, dtype)


def dot(left, right, dims=NN):
    return lax.dot_general(left, right, dims, preferred_element_type=F32)


def one_hot(rows, line):
    places = lax.broadcasted_iota(jnp.int32, (rows, line.shape[1]), 0)
    return jnp.where(places == line, 1.0, 0.0).astype(BF)


def table_kernel(now_ref, out_ref):
    for part in range(3):
        out_ref[pl.ds(part * LANES, LANES), :] = now_ref[part].T.astype(BF)


def request_kernel(slabs, owner_ref, nodes_ref, request_ref, slot_ref):
    request_ref[...] = jnp.zeros_like(request_ref)

    def step(block, counts):
        owner = owner_ref[block]
        rank = jnp.int32(0)
        for slab in range(slabs):
            rank = jnp.where(owner == slab, counts[slab], rank)
        slot = owner * CAP + rank
        slot_ref[block] = slot
        request_ref[pl.ds(slot, 1), :] = nodes_ref[pl.ds(block, 1), :]
        return tuple(counts[slab] + (owner == slab).astype(jnp.int32) for slab in range(slabs))

    lax.fori_loop(0, nodes_ref.shape[0], step, (jnp.int32(0),) * slabs)


def stress_of(full, shear, bulk):
    cofactor = [
        [
            full[(a + 1) % 3][(b + 1) % 3] * full[(a + 2) % 3][(b + 2) % 3]
            - full[(a + 1) % 3][(b + 2) % 3] * full[(a + 2) % 3][(b + 1) % 3]
            for b in range(3)
        ]
        for a in range(3)
    ]
    volume = (
        full[0][0] * cofactor[0][0] + full[0][1] * cofactor[0][1] + full[0][2] * cofactor[0][2]
    )
    clamped = jnp.maximum(volume, 0.3)
    factor = (bulk * jnp.log(clamped) - shear) / clamped
    return [[shear * full[a][b] + factor * cofactor[a][b] for b in range(3)] for a in range(3)]


def cell_kernel(
    low_ref, own_ref, high_ref, nodes_ref, grads_ref, weights_ref, shear_ref, bulk_ref,
    out_ref, total_ref,
):
    step = pl.program_id(0)

    @pl.when(step == 0)
    def _():
        total_ref[...] = jnp.zeros_like(total_ref)

    nodes = nodes_ref[0]
    count = nodes.shape[1]
    cells, _, support, points = grads_ref.shape
    rows = own_ref.shape[1]
    hot = one_hot(3 * rows, nodes >> 7)
    table = jnp.concatenate([low_ref[...], own_ref[...], high_ref[...]], axis=1)
    picked = dot(table, hot)
    low_place = lax.broadcasted_iota(jnp.int32, (LANES, count), 0)
    mask = low_place == (nodes & (LANES - 1))
    cell_mask = (
        lax.broadcasted_iota(jnp.int32, (cells, count), 1) // support
        == lax.broadcasted_iota(jnp.int32, (cells, count), 0)
    )
    left = jnp.concatenate(
        [
            jnp.where(
                cell_mask,
                jnp.sum(
                    jnp.where(mask, picked[part * LANES : (part + 1) * LANES], 0.0),
                    axis=0,
                    keepdims=True,
                ),
                0.0,
            )
            for part in range(3)
        ],
        axis=0,
    ).astype(BF)
    slopes = [grads_ref[:, axis].reshape(count, points) for axis in range(3)]
    grad = [dot(left, slopes[axis]) for axis in range(3)]
    full = [
        [
            grad[b][a * cells : (a + 1) * cells] + (1.0 if a == b else 0.0)
            for b in range(3)
        ]
        for a in range(3)
    ]
    stress = stress_of(full, shear_ref[...], bulk_ref[...])
    weights = weights_ref[...]
    back = None
    for axis in range(3):
        wide = jnp.concatenate([weights * stress[a][axis] for a in range(3)], axis=0).astype(BF)
        term = dot(wide, slopes[axis], NT)
        back = term if back is None else back + term
    scattered = []
    for part in range(3):
        line = jnp.sum(
            jnp.where(cell_mask, back[part * cells : (part + 1) * cells], 0.0),
            axis=0,
            keepdims=True,
        )
        scattered.append(jnp.where(mask, line, 0.0).astype(BF))
    total_ref[...] += dot(jnp.concatenate(scattered, axis=0), hot, NT)

    @pl.when(step == pl.num_programs(0) - 1)
    def _():
        for part in range(3):
            plane = total_ref[pl.ds(part * LANES, LANES), :]
            for slab in range(3):
                out_ref[slab, part] = plane[:, slab * rows : (slab + 1) * rows].T.astype(BF)


def combine_kernel(quarters, place_ref, own_ref, up_ref, down_ref, *outs):
    depth = own_ref.shape[1] // quarters
    for shift in range(quarters):
        first = lax.rem(place_ref[0] + shift, quarters) * depth
        window = pl.ds(pl.multiple_of(first, depth), depth)
        for part in range(3):
            outs[shift][part] = (
                own_ref[part, window, :].astype(F32)
                + up_ref[part, window, :].astype(F32)
                + down_ref[part, window, :].astype(F32)
            ).astype(BF)


def advance_kernel(
    quarters, place_ref, now_ref, prev_ref, mass_ref, *refs
):
    parts, next_ref, send_ref = refs[:quarters], refs[quarters], refs[quarters + 1]
    depth = next_ref.shape[1]
    window = pl.ds(pl.multiple_of(place_ref[0] * depth, depth), depth)
    mass = mass_ref[window, :]
    for part in range(3):
        force = parts[0][part].astype(F32)
        for other in parts[1:]:
            force = force + other[part].astype(F32)
        value = 2.0 * now_ref[part, window, :] - prev_ref[part, window, :] - mass * force
        next_ref[part] = value
        send_ref[part] = value.astype(BF)


def lookup_kernel(quarters, slabs, place_ref, asked_ref, *refs):
    parts, out_ref, table_ref = refs[:quarters], refs[quarters], refs[quarters + 1]
    depth = parts[0].shape[1]
    gathered = refs[quarters + 2]
    for shift in range(quarters):
        owner = lax.rem(place_ref[0] - shift + quarters, quarters)
        window = pl.ds(pl.multiple_of(owner * depth, depth), depth)
        for part in range(3):
            gathered[part, window, :] = parts[shift][part].astype(F32)
    rows = depth * quarters
    for part in range(3):
        table_ref[pl.ds(part * LANES, LANES), :] = gathered[part].T.astype(BF)
    support = asked_ref.shape[2]
    pad = jnp.zeros((out_ref.shape[1] - 3 * CAP, support), F32)

    def step(slab, carry):
        lines = asked_ref[slab]
        low_place = lax.broadcasted_iota(jnp.int32, (LANES, support), 0)
        found = [[], [], []]
        for slot in range(CAP):
            line = lines[slot : slot + 1]
            picked = dot(table_ref[...], one_hot(rows, line >> 7))
            mask = low_place == (line & (LANES - 1))
            for part in range(3):
                found[part].append(
                    jnp.sum(
                        jnp.where(mask, picked[part * LANES : (part + 1) * LANES], 0.0),
                        axis=0,
                        keepdims=True,
                    )
                )
        out_ref[slab] = jnp.concatenate(found[0] + found[1] + found[2] + [pad], axis=0).astype(BF)
        return carry

    lax.fori_loop(0, slabs, step, 0)


def block_kernel(slot_ref, values_ref, phi_ref, corr_ref, target_ref, fixed_ref, out_ref, hold, sent):
    step = pl.program_id(0)
    slabs, height, support = values_ref.shape
    blocks = phi_ref.shape[0]

    @pl.when(step == 0)
    def _():
        for slab in range(slabs):
            hold[slab] = values_ref[slab].astype(F32)
        sent[...] = jnp.zeros_like(sent)

    pad = jnp.zeros((5, support), F32)
    for local in range(blocks):
        slot = slot_ref[step * blocks + local]
        slab, rank = slot // CAP, lax.rem(slot, CAP)
        value = jnp.concatenate(
            [hold[slab, pl.ds(part * CAP + rank, 1), :] for part in range(3)] + [pad], axis=0
        ).astype(BF)
        phi = phi_ref[local].astype(BF)
        interp = dot(value, phi, NT)
        goal = jnp.concatenate([target_ref[local], jnp.zeros((5, phi.shape[0]), F32)], axis=0)
        resid = fixed_ref[local : local + 1].astype(F32) * (goal - interp)
        corr = dot(resid.astype(BF), corr_ref[local].astype(BF), NT)
        delta = dot(corr.astype(BF), phi)
        for part in range(3):
            sent[slab, pl.ds(part * CAP + rank, 1), :] = delta[part : part + 1]

    @pl.when(step == pl.num_programs(0) - 1)
    def _():
        for slab in range(slabs):
            out_ref[slab] = sent[slab].astype(BF)


def spread_kernel(quarters, slabs, place_ref, asked_ref, arrived_ref, *refs):
    outs, total_ref = refs[:quarters], refs[quarters]
    depth = outs[0].shape[1]
    rows = depth * quarters
    support = asked_ref.shape[2]
    total_ref[...] = jnp.zeros_like(total_ref)

    def step(slab, carry):
        lines = asked_ref[slab]
        values = arrived_ref[slab].astype(F32)
        low_place = lax.broadcasted_iota(jnp.int32, (LANES, support), 0)
        wide, hots = [], []
        for slot in range(CAP):
            line = lines[slot : slot + 1]
            mask = low_place == (line & (LANES - 1))
            wide.append(
                jnp.concatenate(
                    [
                        jnp.where(mask, values[part * CAP + slot : part * CAP + slot + 1], 0.0)
                        for part in range(3)
                    ],
                    axis=0,
                ).astype(BF)
            )
            hots.append(one_hot(rows, line >> 7))
        total_ref[...] += dot(jnp.concatenate(wide, axis=1), jnp.concatenate(hots, axis=1), NT)
        return carry

    lax.fori_loop(0, slabs, step, 0)
    natural = refs[quarters + 1]
    for part in range(3):
        natural[part] = total_ref[pl.ds(part * LANES, LANES), :].T
    for shift in range(quarters):
        first = lax.rem(place_ref[0] + shift, quarters) * depth
        window = pl.ds(pl.multiple_of(first, depth), depth)
        for part in range(3):
            outs[shift][part] = natural[part, window, :].astype(BF)


def finish_kernel(next_ref, *refs):
    out_ref = refs[-1]
    for part in range(3):
        value = refs[0][part].astype(F32)
        for other in refs[1:-1]:
            value = value + other[part].astype(F32)
        out_ref[part] = next_ref[part] + value


def gather_kernel(quarters, place_ref, *refs):
    parts, out_ref = refs[:quarters], refs[quarters]
    depth = parts[0].shape[1]
    for shift in range(quarters):
        owner = lax.rem(place_ref[0] - shift + quarters, quarters)
        window = pl.ds(pl.multiple_of(owner * depth, depth), depth)
        for part in range(3):
            out_ref[part, window, :] = parts[shift][part]


def shifted(array, axis, by, wrap):
    size = lax.axis_size(axis)
    if wrap:
        pairs = [(i, (i + by) % size) for i in range(size)]
    else:
        pairs = [(i, i + by) for i in range(size) if 0 <= i + by < size]
    return lax.ppermute(array, axis, pairs)


def body(
    disp_now,
    disp_prev,
    inv_mass,
    cell_nodes,
    shape_grads,
    cell_weights,
    cell_shear,
    cell_bulk,
    block_owner,
    block_nodes,
    block_phi,
    block_corr,
    block_target,
    block_fixed,
):
    width = disp_now.shape[1]
    slabs = lax.axis_size("slab")
    quarters = lax.axis_size("group")
    rows = width // LANES
    depth = rows // quarters
    place = lax.axis_index("group").astype(jnp.int32).reshape(1)
    now = disp_now.reshape(3, rows, LANES)
    prev = disp_prev.reshape(3, rows, LANES)
    mass = inv_mass.reshape(rows, LANES)

    own = call(table_kernel, shape_of((3 * LANES, rows), BF), [VMEM])(now)
    low = shifted(own, "slab", 1, False)
    high = shifted(own, "slab", -1, False)

    blocks, support = block_nodes.shape
    request, slot = call(
        functools.partial(request_kernel, slabs),
        (shape_of((slabs * CAP, support), jnp.int32), shape_of((blocks,), jnp.int32)),
        [SMEM, VMEM],
        (VMEM, SMEM),
    )(block_owner.reshape(blocks), block_nodes)
    asked = lax.all_to_all(
        request.reshape(slabs, CAP, support), "slab", split_axis=0, concat_axis=0, tiled=True
    )

    cells, _, count, points = shape_grads.shape
    steps = cells // GROUP_CELLS
    lines = cell_nodes.reshape(steps, 1, GROUP_CELLS * count)
    partial = pl.pallas_call(
        cell_kernel,
        out_shape=shape_of((3, 3, rows, LANES), BF),
        grid=(steps,),
        in_specs=[
            pl.BlockSpec((3 * LANES, rows), lambda s: (0, 0)),
            pl.BlockSpec((3 * LANES, rows), lambda s: (0, 0)),
            pl.BlockSpec((3 * LANES, rows), lambda s: (0, 0)),
            pl.BlockSpec((1, 1, GROUP_CELLS * count), lambda s: (s, 0, 0)),
            pl.BlockSpec((GROUP_CELLS, 3, count, points), lambda s: (s, 0, 0, 0)),
            pl.BlockSpec((GROUP_CELLS, points), lambda s: (s, 0)),
            pl.BlockSpec((GROUP_CELLS, 1), lambda s: (s, 0)),
            pl.BlockSpec((GROUP_CELLS, 1), lambda s: (s, 0)),
        ],
        out_specs=pl.BlockSpec((3, 3, rows, LANES), lambda s: (0, 0, 0, 0)),
        scratch_shapes=[pltpu.VMEM((3 * LANES, 3 * rows), F32)],
        compiler_params=PARAMS,
    )(
        low, own, high, lines, shape_grads, cell_weights,
        cell_shear.reshape(cells, 1), cell_bulk.reshape(cells, 1),
    )

    from_above = shifted(partial[0], "slab", -1, False)
    from_below = shifted(partial[2], "slab", 1, False)
    quarter = (3, depth, LANES)
    pieces = call(
        functools.partial(combine_kernel, quarters),
        (shape_of(quarter, BF),) * quarters,
        [SMEM] + [VMEM] * 3,
    )(place, partial[1], from_above, from_below)
    pieces = [pieces[0]] + [
        shifted(pieces[by], "group", by, True) for by in range(1, quarters)
    ]
    mine, sent = call(
        functools.partial(advance_kernel, quarters),
        (shape_of(quarter, F32), shape_of(quarter, BF)),
        [SMEM] + [VMEM] * (3 + quarters),
    )(place, now, prev, mass, *pieces)
    tables = [sent] + [shifted(sent, "group", by, True) for by in range(1, quarters)]
    height = -(-3 * CAP // 16) * 16
    looked = call(
        functools.partial(lookup_kernel, quarters, slabs),
        shape_of((slabs, height, support), BF),
        [SMEM] + [VMEM] * (1 + quarters),
        scratch_shapes=[
            pltpu.VMEM((3 * LANES, rows), BF),
            pltpu.VMEM((3, rows, LANES), F32),
        ],
    )(place, asked, *tables)
    values = lax.all_to_all(looked, "slab", split_axis=0, concat_axis=0, tiled=True)

    each = 8
    border = block_phi.shape[1]
    outgoing = pl.pallas_call(
        block_kernel,
        out_shape=shape_of((slabs, height, support), BF),
        grid=(blocks // each,),
        in_specs=[
            SMEM,
            pl.BlockSpec((slabs, height, support), lambda s: (0, 0, 0)),
            pl.BlockSpec((each, border, support), lambda s: (s, 0, 0)),
            pl.BlockSpec((each, border, border), lambda s: (s, 0, 0)),
            pl.BlockSpec((each, 3, border), lambda s: (s, 0, 0)),
            pl.BlockSpec((each, border), lambda s: (s, 0)),
        ],
        out_specs=pl.BlockSpec((slabs, height, support), lambda s: (0, 0, 0)),
        scratch_shapes=[
            pltpu.VMEM((slabs, height, support), F32),
            pltpu.VMEM((slabs, height, support), F32),
        ],
        compiler_params=PARAMS,
    )(slot, values, block_phi, block_corr, block_target, block_fixed)
    arrived = lax.all_to_all(outgoing, "slab", split_axis=0, concat_axis=0, tiled=True)
    added = call(
        functools.partial(spread_kernel, quarters, slabs),
        (shape_of(quarter, BF),) * quarters,
        [SMEM] + [VMEM] * 2,
        scratch_shapes=[
            pltpu.VMEM((3 * LANES, rows), F32),
            pltpu.VMEM((3, rows, LANES), F32),
        ],
    )(place, asked, arrived)
    added = [added[0]] + [shifted(added[by], "group", by, True) for by in range(1, quarters)]
    final = call(finish_kernel, shape_of(quarter, F32), [VMEM] * (1 + quarters))(mine, *added)
    finals = [final] + [shifted(final, "group", by, True) for by in range(1, quarters)]
    whole = call(
        functools.partial(gather_kernel, quarters),
        shape_of((3, rows, LANES), F32),
        [SMEM] + [VMEM] * quarters,
    )(place, *finals)
    return whole.reshape(3, width)


def solution(mesh):
    placed = (
        P(None, "slab"),
        P(None, "slab"),
        P("slab"),
        P(("slab", "group"), None),
        P(("slab", "group"), None, None, None),
        P(("slab", "group"), None),
        P(("slab", "group")),
        P(("slab", "group")),
        P(("slab", "group"), None),
        P(("slab", "group"), None),
        P(("slab", "group"), None, None),
        P(("slab", "group"), None, None),
        P(("slab", "group"), None, None),
        P(("slab", "group"), None),
    )
    return jax.shard_map(
        body, mesh=mesh, in_specs=placed, out_specs=P(None, "slab"), check_vma=False
    )
```

```python
import functools

import jax
import jax.numpy as jnp
from jax import lax
from jax.experimental import pallas as pl
from jax.experimental.pallas import tpu as pltpu
from jax.sharding import PartitionSpec as P

CAP = 4
LANES = 128
GROUP_CELLS = 8
CHUNK = 256
EACH = 8
BF = jnp.bfloat16
F32 = jnp.float32
VMEM = pl.BlockSpec(memory_space=pltpu.VMEM)
SMEM = pl.BlockSpec(memory_space=pltpu.SMEM)
PARAMS = pltpu.CompilerParams(vmem_limit_bytes=32 * 1024 * 1024)
NT = (((1,), (1,)), ((), ()))
NN = (((1,), (0,)), ((), ()))


def pinned(array):
    return pltpu.with_memory_space_constraint(array, pltpu.VMEM)


def call(kernel, outs, in_specs, out_specs=None, **extra):
    many = isinstance(outs, tuple)
    specs = out_specs if out_specs is not None else ((VMEM,) * len(outs) if many else VMEM)
    run = pl.pallas_call(
        kernel,
        out_shape=outs,
        in_specs=in_specs,
        out_specs=specs,
        compiler_params=PARAMS,
        **extra,
    )

    def placed(*arrays):
        return run(
            *(
                pinned(array) if spec is VMEM else array
                for array, spec in zip(arrays, in_specs, strict=True)
            )
        )

    return placed


def shape_of(dims, dtype):
    return pltpu.VMEM(dims, dtype)


def dot(left, right, dims=NN):
    return lax.dot_general(left, right, dims, preferred_element_type=F32)


def one_hot(rows, line):
    places = lax.broadcasted_iota(jnp.int32, (rows, line.shape[1]), 0).astype(jnp.int16)
    return jnp.where(places == line.astype(jnp.int16), jnp.ones((), BF), jnp.zeros((), BF))


def chosen(picked, low):
    spots = lax.broadcasted_iota(jnp.int32, (8, low.shape[1]), 0)
    kept = [None] * 3
    for start in range(0, LANES, 8):
        mask = spots == low - start
        for part in range(3):
            piece = picked[part * LANES + start : part * LANES + start + 8]
            rest = 0.0 if kept[part] is None else kept[part]
            kept[part] = jnp.where(mask, piece, rest)
    return [jnp.sum(each, axis=0, keepdims=True) for each in kept]


def spread_rows(lines, low):
    spots = lax.broadcasted_iota(jnp.int32, (LANES, low.shape[1]), 0).astype(jnp.int16)
    mask = spots == low.astype(jnp.int16)
    return jnp.concatenate(
        [
            jnp.where(mask, jnp.broadcast_to(line.astype(BF), mask.shape), jnp.zeros((), BF))
            for line in lines
        ],
        axis=0,
    )


def front_kernel(slabs, owner_ref, now_ref, nodes_ref, table_ref, request_ref, slot_ref):
    for part in range(3):
        table_ref[pl.ds(part * LANES, LANES), :] = now_ref[:, part, :].T.astype(BF)
    request_ref[...] = jnp.zeros_like(request_ref)

    def step(block, counts):
        owner = owner_ref[block]
        rank = jnp.int32(0)
        for slab in range(slabs):
            rank = jnp.where(owner == slab, counts[slab], rank)
        slot_ref[block] = owner * CAP + rank
        request_ref[owner, pl.ds(rank, 1), :] = nodes_ref[pl.ds(block, 1), :]
        return tuple(counts[slab] + (owner == slab).astype(jnp.int32) for slab in range(slabs))

    lax.fori_loop(0, nodes_ref.shape[0], step, (jnp.int32(0),) * slabs)


def stress_of(full, shear, bulk):
    cofactor = [
        [
            full[(a + 1) % 3][(b + 1) % 3] * full[(a + 2) % 3][(b + 2) % 3]
            - full[(a + 1) % 3][(b + 2) % 3] * full[(a + 2) % 3][(b + 1) % 3]
            for b in range(3)
        ]
        for a in range(3)
    ]
    volume = (
        full[0][0] * cofactor[0][0] + full[0][1] * cofactor[0][1] + full[0][2] * cofactor[0][2]
    )
    clamped = jnp.maximum(volume, 0.3)
    factor = (bulk * jnp.log(clamped) - shear) / clamped
    return [[shear * full[a][b] + factor * cofactor[a][b] for b in range(3)] for a in range(3)]


def cell_kernel(
    low_ref, own_ref, high_ref, nodes_ref, grads_ref, weights_ref, shear_ref, bulk_ref,
    down_ref, stay_ref, up_ref, total_ref, table_ref,
):
    cells, _, support, points = grads_ref.shape
    rows = own_ref.shape[1]
    each = GROUP_CELLS
    count = each * support
    for place, ref in enumerate((low_ref, own_ref, high_ref)):
        table_ref[:, place * rows : (place + 1) * rows] = ref[...]
    cell_mask = (
        lax.broadcasted_iota(jnp.int32, (each, count), 1) // support
        == lax.broadcasted_iota(jnp.int32, (each, count), 0)
    )
    spot = lax.broadcasted_iota(jnp.int32, (each, 1), 0)
    for base in range(0, cells, each):
        nodes = jnp.concatenate(
            [nodes_ref[base + cell : base + cell + 1, :] for cell in range(each)], axis=1
        )
        high, low = nodes >> 7, nodes & (LANES - 1)
        found = [[], [], []]
        for start in range(0, count, CHUNK):
            part = slice(start, start + CHUNK)
            picked = dot(table_ref[...], one_hot(3 * rows, high[:, part]))
            for held, line in zip(found, chosen(picked, low[:, part])):
                held.append(line)
        left = jnp.concatenate(
            [jnp.where(cell_mask, jnp.concatenate(held, axis=1), 0.0) for held in found], axis=0
        ).astype(BF)
        slopes = [grads_ref[base : base + each, axis].reshape(count, points) for axis in range(3)]
        grad = [dot(left, slopes[axis]) for axis in range(3)]
        full = [
            [grad[b][a * each : (a + 1) * each] + (1.0 if a == b else 0.0) for b in range(3)]
            for a in range(3)
        ]
        shear = jnp.zeros((each, 1), F32)
        bulk = jnp.zeros((each, 1), F32)
        for cell in range(each):
            shear = jnp.where(spot == cell, shear_ref[base + cell], shear)
            bulk = jnp.where(spot == cell, bulk_ref[base + cell], bulk)
        stress = stress_of(full, shear, bulk)
        weights = weights_ref[base : base + each, :]
        back = None
        for axis in range(3):
            wide = jnp.concatenate([weights * stress[a][axis] for a in range(3)], axis=0)
            term = dot(wide.astype(BF), slopes[axis], NT)
            back = term if back is None else back + term
        lines = [
            jnp.sum(
                jnp.where(cell_mask, back[a * each : (a + 1) * each], 0.0), axis=0, keepdims=True
            )
            for a in range(3)
        ]
        term = dot(spread_rows(lines, low), one_hot(3 * rows, high), NT)
        total_ref[...] = term if base == 0 else total_ref[...] + term
    for part in range(3):
        plane = total_ref[pl.ds(part * LANES, LANES), :]
        for place, ref in enumerate((down_ref, stay_ref, up_ref)):
            ref[part] = plane[:, place * rows : (place + 1) * rows].T.astype(BF)


def combine_kernel(quarters, place_ref, own_ref, up_ref, down_ref, *outs):
    depth = own_ref.shape[1] // quarters
    for shift in range(quarters):
        first = lax.rem(place_ref[0] + shift, quarters) * depth
        window = pl.ds(pl.multiple_of(first, depth), depth)
        for part in range(3):
            outs[shift][part] = (
                own_ref[part, window, :].astype(F32)
                + up_ref[part, window, :].astype(F32)
                + down_ref[part, window, :].astype(F32)
            ).astype(BF)


def advance_kernel(
    quarters, place_ref, now_ref, prev_ref, mass_ref, *refs
):
    parts, next_ref, send_ref = refs[:quarters], refs[quarters], refs[quarters + 1]
    depth = next_ref.shape[1]
    window = pl.ds(pl.multiple_of(place_ref[0] * depth, depth), depth)
    mass = mass_ref[window, :]
    for part in range(3):
        force = parts[0][part].astype(F32)
        for other in parts[1:]:
            force = force + other[part].astype(F32)
        value = 2.0 * now_ref[window, part, :] - prev_ref[window, part, :] - mass * force
        next_ref[part] = value
        send_ref[part] = value.astype(BF)


def lookup_kernel(quarters, slabs, place_ref, asked_ref, *refs):
    parts, out_ref, table_ref = refs[:quarters], refs[quarters], refs[quarters + 1]
    depth = parts[0].shape[1]
    gathered = refs[quarters + 2]
    for shift in range(quarters):
        owner = lax.rem(place_ref[0] - shift + quarters, quarters)
        window = pl.ds(pl.multiple_of(owner * depth, depth), depth)
        for part in range(3):
            gathered[part, window, :] = parts[shift][part].astype(F32)
    rows = depth * quarters
    for part in range(3):
        table_ref[pl.ds(part * LANES, LANES), :] = gathered[part].T.astype(BF)
    support = asked_ref.shape[2]
    pad = jnp.zeros((out_ref.shape[1] - 3 * CAP, support), F32)

    def step(slab, carry):
        lines = asked_ref[slab]
        found = [[], [], []]
        for slot in range(CAP):
            line = lines[slot : slot + 1]
            picked = dot(table_ref[...], one_hot(rows, line >> 7))
            for held, each in zip(found, chosen(picked, line & (LANES - 1))):
                held.append(each)
        out_ref[slab] = jnp.concatenate(found[0] + found[1] + found[2] + [pad], axis=0).astype(BF)
        return carry

    lax.fori_loop(0, slabs, step, 0, unroll=4)


def block_kernel(
    slot_ref, values_ref, phi_ref, corr_ref, target_ref, fixed_ref, out_ref, hold, sent
):
    slabs, height, support = values_ref.shape
    blocks = phi_ref.shape[0]
    for slab in range(slabs):
        hold[slab] = values_ref[slab].astype(F32)
    sent[...] = jnp.zeros_like(sent)
    pad = jnp.zeros((5, support), F32)

    def step(turn, carry):
        places, phis, works = [], [], []
        for local in range(EACH):
            block = turn * EACH + local
            slot = slot_ref[block]
            slab, rank = slot // CAP, lax.rem(slot, CAP)
            places.append((block, slab, rank))
            works.append(
                jnp.concatenate(
                    [hold[slab, pl.ds(part * CAP + rank, 1), :] for part in range(3)] + [pad],
                    axis=0,
                ).astype(BF)
            )
            phis.append(phi_ref[block].astype(BF))
        works = [dot(work, phi, NT) for work, phi in zip(works, phis)]
        resids = []
        for (block, _, _), interp in zip(places, works):
            goal = jnp.concatenate(
                [target_ref[block], jnp.zeros((5, interp.shape[1]), F32)], axis=0
            )
            fixed = fixed_ref[pl.ds(block, 1), :].astype(F32)
            resids.append((fixed * (goal - interp)).astype(BF))
        works = [
            dot(resid, corr_ref[block].astype(BF), NT)
            for (block, _, _), resid in zip(places, resids)
        ]
        works = [dot(corr.astype(BF), phi) for corr, phi in zip(works, phis)]
        for (_, slab, rank), delta in zip(places, works):
            for part in range(3):
                sent[slab, pl.ds(part * CAP + rank, 1), :] = delta[part : part + 1]
        return carry

    lax.fori_loop(0, blocks // EACH, step, 0)
    for slab in range(slabs):
        out_ref[slab] = sent[slab].astype(BF)


def spread_kernel(quarters, slabs, place_ref, asked_ref, arrived_ref, *refs):
    outs, total_ref = refs[:quarters], refs[quarters]
    depth = outs[0].shape[1]
    rows = depth * quarters
    for slab in range(slabs):
        lines = asked_ref[slab]
        values = arrived_ref[slab].astype(F32)
        wide, hots = [], []
        for slot in range(CAP):
            line = lines[slot : slot + 1]
            picks = [values[part * CAP + slot : part * CAP + slot + 1] for part in range(3)]
            wide.append(spread_rows(picks, line & (LANES - 1)))
            hots.append(one_hot(rows, line >> 7))
        term = dot(jnp.concatenate(wide, axis=1), jnp.concatenate(hots, axis=1), NT)
        total_ref[...] = term if slab == 0 else total_ref[...] + term
    natural = refs[quarters + 1]
    for part in range(3):
        natural[part] = total_ref[pl.ds(part * LANES, LANES), :].T
    for shift in range(quarters):
        first = lax.rem(place_ref[0] + shift, quarters) * depth
        window = pl.ds(pl.multiple_of(first, depth), depth)
        for part in range(3):
            outs[shift][part] = natural[part, window, :].astype(BF)


def finish_kernel(next_ref, *refs):
    out_ref = refs[-1]
    for part in range(3):
        value = refs[0][part].astype(F32)
        for other in refs[1:-1]:
            value = value + other[part].astype(F32)
        out_ref[part] = (next_ref[part] + value).astype(BF)


def gather_kernel(quarters, place_ref, *refs):
    parts, out_ref = refs[:quarters], refs[quarters]
    depth = parts[0].shape[1]
    for shift in range(quarters):
        owner = lax.rem(place_ref[0] - shift + quarters, quarters)
        window = pl.ds(pl.multiple_of(owner * depth, depth), depth)
        for part in range(3):
            out_ref[window, part, :] = parts[shift][part].astype(F32)


def shifted(array, axis, by, wrap):
    size = lax.axis_size(axis)
    if wrap:
        pairs = [(i, (i + by) % size) for i in range(size)]
    else:
        pairs = [(i, i + by) for i in range(size) if 0 <= i + by < size]
    return lax.ppermute(array, axis, pairs)


def body(
    disp_now,
    disp_prev,
    inv_mass,
    cell_nodes,
    shape_grads,
    cell_weights,
    cell_shear,
    cell_bulk,
    block_owner,
    block_nodes,
    block_phi,
    block_corr,
    block_target,
    block_fixed,
):
    width = disp_now.shape[1]
    slabs = lax.axis_size("slab")
    quarters = lax.axis_size("group")
    rows = width // LANES
    depth = rows // quarters
    place = lax.axis_index("group").astype(jnp.int32).reshape(1)
    now = jnp.transpose(disp_now.reshape(3, rows, LANES), (1, 0, 2))
    prev = jnp.transpose(disp_prev.reshape(3, rows, LANES), (1, 0, 2))
    mass = inv_mass.reshape(rows, LANES)
    blocks, support = block_nodes.shape

    own, request, slot = call(
        functools.partial(front_kernel, slabs),
        (
            shape_of((3 * LANES, rows), BF),
            shape_of((slabs, CAP, support), jnp.int32),
            jax.ShapeDtypeStruct((blocks,), jnp.int32),
        ),
        [SMEM, VMEM, VMEM],
        (VMEM, VMEM, SMEM),
    )(block_owner.reshape(blocks), now, block_nodes)
    low = shifted(own, "slab", 1, False)
    high = shifted(own, "slab", -1, False)
    asked = lax.all_to_all(request, "slab", split_axis=0, concat_axis=0, tiled=True)

    down, stay, up = call(
        cell_kernel,
        (shape_of((3, rows, LANES), BF),) * 3,
        [VMEM] * 6 + [SMEM] * 2,
        scratch_shapes=[
            pltpu.VMEM((3 * LANES, 3 * rows), F32),
            pltpu.VMEM((3 * LANES, 3 * rows), BF),
        ],
    )(low, own, high, cell_nodes, shape_grads, cell_weights, cell_shear, cell_bulk)

    from_above = shifted(down, "slab", -1, False)
    from_below = shifted(up, "slab", 1, False)
    quarter = (3, depth, LANES)
    pieces = call(
        functools.partial(combine_kernel, quarters),
        (shape_of(quarter, BF),) * quarters,
        [SMEM] + [VMEM] * 3,
    )(place, stay, from_above, from_below)
    pieces = [pieces[0]] + [
        shifted(pieces[by], "group", by, True) for by in range(1, quarters)
    ]
    mine, sent = call(
        functools.partial(advance_kernel, quarters),
        (shape_of(quarter, F32), shape_of(quarter, BF)),
        [SMEM] + [VMEM] * (3 + quarters),
    )(place, now, prev, mass, *pieces)
    tables = [sent] + [shifted(sent, "group", by, True) for by in range(1, quarters)]
    height = -(-3 * CAP // 16) * 16
    looked = call(
        functools.partial(lookup_kernel, quarters, slabs),
        shape_of((slabs, height, support), BF),
        [SMEM] + [VMEM] * (1 + quarters),
        scratch_shapes=[
            pltpu.VMEM((3 * LANES, rows), BF),
            pltpu.VMEM((3, rows, LANES), F32),
        ],
    )(place, asked, *tables)
    values = lax.all_to_all(looked, "slab", split_axis=0, concat_axis=0, tiled=True)

    outgoing = call(
        block_kernel,
        shape_of((slabs, height, support), BF),
        [SMEM] + [VMEM] * 5,
        scratch_shapes=[
            pltpu.VMEM((slabs, height, support), F32),
            pltpu.VMEM((slabs, height, support), F32),
        ],
    )(slot, values, block_phi, block_corr, block_target, block_fixed)
    arrived = lax.all_to_all(outgoing, "slab", split_axis=0, concat_axis=0, tiled=True)
    added = call(
        functools.partial(spread_kernel, quarters, slabs),
        (shape_of(quarter, BF),) * quarters,
        [SMEM] + [VMEM] * 2,
        scratch_shapes=[
            pltpu.VMEM((3 * LANES, rows), F32),
            pltpu.VMEM((3, rows, LANES), F32),
        ],
    )(place, asked, arrived)
    added = [added[0]] + [shifted(added[by], "group", by, True) for by in range(1, quarters)]
    final = call(finish_kernel, shape_of(quarter, BF), [VMEM] * (1 + quarters))(mine, *added)
    finals = [final] + [shifted(final, "group", by, True) for by in range(1, quarters)]
    whole = call(
        functools.partial(gather_kernel, quarters),
        shape_of((rows, 3, LANES), F32),
        [SMEM] + [VMEM] * quarters,
    )(place, *finals)
    return jnp.transpose(whole, (1, 0, 2)).reshape(3, width)


def solution(mesh):
    placed = (
        P(None, "slab"),
        P(None, "slab"),
        P("slab"),
        P(("slab", "group"), None),
        P(("slab", "group"), None, None, None),
        P(("slab", "group"), None),
        P(("slab", "group")),
        P(("slab", "group")),
        P(("slab", "group"), None),
        P(("slab", "group"), None),
        P(("slab", "group"), None, None),
        P(("slab", "group"), None, None),
        P(("slab", "group"), None, None),
        P(("slab", "group"), None),
    )
    return jax.shard_map(
        body, mesh=mesh, in_specs=placed, out_specs=P(None, "slab"), check_vma=False
    )
```
